32 devices in a mesh: fsdp: 8 (over z, x), tp: 4 (over y, core).
Axes of the slice: x: 2, y: 2, z: 4, core: 2. Of those that a mesh axis runs over, the one named last changes fastest.
Arguments:
- step_input: bfloat16 [4, 768, 8192], P(None, 'fsdp'), may hold values from -6 to 6
- lengths: int32 [768], P('fsdp'), may hold values from 1 to 128, as said below
- cache_k: bfloat16 [768, 128, 1024], P('fsdp', None, 'tp'), may hold values from -500 to 500
- cache_v: bfloat16 [768, 128, 1024], P('fsdp', None, 'tp'), may hold values from -6 to 6
- w_query: bfloat16 [8192, 4096], P('fsdp', 'tp'), may hold values from -0.0625 to 0.0625
- w_key: bfloat16 [8192, 1024], P('fsdp', 'tp'), may hold values from -0.0625 to 0.0625
- w_value: bfloat16 [8192, 1024], P('fsdp', 'tp'), may hold values from -0.0625 to 0.0625
- w_output: bfloat16 [4096, 8192], P('fsdp', 'tp'), may hold values from -0.09375 to 0.09375
- loss_grad: bfloat16 [4, 768, 8192], P(None, 'fsdp', 'tp'), may hold values from -6 to 6
Outputs:
- layer_out: bfloat16 [4, 768, 8192], P(None, 'fsdp', 'tp')
- grad_output: float32 [4096, 8192], P('fsdp', 'tp')
The draws below stay inside these ranges and needn't reach their ends.
Inputs may be any that keep to these rules, and one draw needn't show every extreme that they name: `lengths`: every row has at least one filled position; some row in every draw is full (128).
All inputs are finite; a program needn't handle non-finite values.
Results may differ from the reference program's by a relative error of at most 0.008.
The reference program's roundings to bfloat16 on the way count: a program that leaves them out, or rounds other values in their place, can miss the bound.
Values may be sent and summed in bfloat16 or wider, within the bound.
A program may use at most 128 MiB of HBM per device.

```python
import jax
import jax.numpy as jnp
from jax import lax

D = 8192
QH = 32
KVH = 8
HD = 128
STEPS = 4
CACHE = 128
ROWS = 768


def draw_lengths(key, part):
    first, second = jax.random.split(jax.random.fold_in(key, 11))
    filled = jax.random.randint(first, (ROWS,), 1, CACHE + 1)
    chosen = jax.random.randint(second, (), 0, ROWS)
    return filled.at[chosen].set(CACHE).astype(jnp.int32)


def draw_cache_k(key, part):
    first = jax.random.fold_in(jax.random.fold_in(key, 23), 0)
    base = jax.random.normal(first, (ROWS, CACHE, KVH * HD), jnp.float32)
    return jnp.clip(base, -500.0, 500.0).astype(jnp.bfloat16)


def levels(key, dims, cuts, low, largest):
    loudness = 1.0
    for position, shards_of in cuts:
        draws = jax.random.uniform(jax.random.fold_in(jax.random.fold_in(key, 6), position), (shards_of,), jnp.float32, low / len(cuts), largest / len(cuts))
        loudness = loudness * jnp.repeat(jnp.exp(draws), dims[position] // shards_of).reshape((-1,) + (1,) * (len(dims) - 1 - position))
    return loudness


def gaussian(key, extent, scale, bound, shards=(), kind=jnp.bfloat16):
    result = jax.random.normal(key, extent, jnp.float32) * scale
    if len(shards) > 0:
        result = levels(key, extent, shards, -0.22, 0.18) * result
    return jnp.clip(result, min=-bound, max=bound).astype(kind)


def setup_inputs(seed: int = 0) -> dict:
    splits = jax.random.split(jax.random.key(seed), 10)
    return {
        "step_input": gaussian(splits[0], (STEPS, ROWS, D), 1.0, 6.0, ((1, 8),)),
        "lengths": draw_lengths(jax.random.fold_in(splits[9], 71), 0),
        "cache_k": draw_cache_k(jax.random.fold_in(splits[9], 71), 0),
        "cache_v": gaussian(splits[3], (ROWS, CACHE, KVH * HD), 1.0, 6.0, ((0, 8), (2, 4))),
        "w_query": gaussian(splits[4], (D, QH * HD), D ** -0.5, 0.0625, ((0, 8), (1, 4))),
        "w_key": gaussian(splits[5], (D, KVH * HD), D ** -0.5, 0.0625, ((0, 8), (1, 4))),
        "w_value": gaussian(splits[6], (D, KVH * HD), D ** -0.5, 0.0625, ((0, 8), (1, 4))),
        "w_output": gaussian(splits[7], (QH * HD, D), (QH * HD) ** -0.5, 0.09375, ((0, 8), (1, 4))),
        "loss_grad": gaussian(splits[8], (STEPS, ROWS, D), 1.0, 6.0, ((1, 8), (2, 4))),
    }


rope_base = 1000000.0


def rotate(vec, pos):
    half = vec.shape[-1] // 2
    freq = rope_base ** (-(jnp.arange(half).astype(jnp.float32) * 2.0) / vec.shape[-1])
    angle = pos[..., None] * freq
    cosine = jnp.cos(angle)
    sine = jnp.sin(angle)
    first = vec[..., :half]
    second = vec[..., half:]
    return jnp.concatenate([first * cosine - second * sine, second * cosine + first * sine], axis=-1)


def reference(step_input, lengths, cache_k, cache_v, w_query, w_key, w_value, w_output, loss_grad):
    steps, rows, width = step_input.shape
    flat = step_input.reshape(steps * rows, width)
    query = jnp.dot(flat, w_query, preferred_element_type=jnp.float32).reshape(steps, rows, QH, HD)
    key = jnp.dot(flat, w_key, preferred_element_type=jnp.float32).reshape(steps, rows, KVH, HD)
    value = jnp.dot(flat, w_value, preferred_element_type=jnp.float32).reshape(steps, rows, KVH, HD)
    pos = lengths.astype(jnp.float32)[None, :] + jnp.arange(steps).astype(jnp.float32)[:, None]
    q_rot = rotate(query, pos[:, :, None]).astype(jnp.bfloat16)
    k_new = rotate(key, pos[:, :, None]).astype(jnp.bfloat16)
    v_new = value.astype(jnp.bfloat16)
    group = QH // KVH
    cache_len = cache_k.shape[1]
    qg = q_rot.reshape(steps, rows, KVH, group, HD).astype(jnp.float32)
    kc = cache_k.reshape(rows, cache_len, KVH, HD).astype(jnp.float32)
    vc = cache_v.reshape(rows, cache_len, KVH, HD).astype(jnp.float32)
    scale = 1.0 / (HD ** 0.5)
    s_cache = jnp.einsum('srhgd,rchd->srhgc', qg, kc) * scale
    s_new = jnp.einsum('srhgd,trhd->srhgt', qg, k_new.astype(jnp.float32)) * scale
    valid = (jnp.arange(cache_len)[None, :] < lengths[:, None])[None, :, None, None, :]
    causal = (jnp.arange(steps)[None, :] <= jnp.arange(steps)[:, None])[:, None, None, None, :]
    s_cache = jnp.where(valid, s_cache, -1e30)
    s_new = jnp.where(causal, s_new, -1e30)
    top = jnp.maximum(jnp.max(s_cache, axis=-1), jnp.max(s_new, axis=-1))[..., None]
    e_cache = jnp.where(valid, jnp.exp(s_cache - top), 0.0)
    e_new = jnp.where(causal, jnp.exp(s_new - top), 0.0)
    total = jnp.sum(e_cache, axis=-1, keepdims=True) + jnp.sum(e_new, axis=-1, keepdims=True)
    p_cache = (e_cache / total).astype(jnp.bfloat16).astype(jnp.float32)
    p_new = (e_new / total).astype(jnp.bfloat16).astype(jnp.float32)
    out = jnp.einsum('srhgc,rchd->srhgd', p_cache, vc) + jnp.einsum('srhgt,trhd->srhgd', p_new, v_new.astype(jnp.float32))
    attended = out.astype(jnp.bfloat16).reshape(steps * rows, QH * HD)
    layer_out = jnp.dot(attended, w_output, preferred_element_type=jnp.float32).astype(jnp.bfloat16).reshape(steps, rows, width)
    grad_output = lax.dot_general(attended, loss_grad.reshape(steps * rows, width), (((0,), (0,)), ((), ())), preferred_element_type=jnp.float32)
    return layer_out, grad_output
```

```python
import functools

import jax
import jax.numpy as jnp
from jax import lax
from jax.experimental import pallas as pl
from jax.experimental.pallas import tpu as pltpu
from jax.sharding import PartitionSpec as P

HD = 128


rope_base = 1000000.0


def rotate(vec, pos):
    half = vec.shape[-1] // 2
    freq = rope_base ** (-(jnp.arange(half).astype(jnp.float32) * 2.0) / vec.shape[-1])
    angle = pos[..., None] * freq
    cosine = jnp.cos(angle)
    sine = jnp.sin(angle)
    first = vec[..., :half]
    second = vec[..., half:]
    return jnp.concatenate(
        [first * cosine - second * sine, second * cosine + first * sine], axis=-1
    )


def attend(q_rot, k_new, v_new, cache_k, cache_v, lengths, kv_local, group):
    steps, rows = (q_rot.shape[0], q_rot.shape[1])
    head_size = q_rot.shape[-1]
    cache_len = cache_k.shape[1]
    qg = q_rot.reshape(steps, rows, kv_local, group, head_size)
    kc = cache_k.reshape(rows, cache_len, kv_local, head_size)
    vc = cache_v.reshape(rows, cache_len, kv_local, head_size)
    scale = 1.0 / head_size**0.5
    s_cache = jnp.einsum("srhgd,rchd->srhgc", qg, kc, preferred_element_type=jnp.float32) * scale
    s_new = jnp.einsum("srhgd,trhd->srhgt", qg, k_new, preferred_element_type=jnp.float32) * scale
    valid = (jnp.arange(cache_len)[None, :] < lengths[:, None])[None, :, None, None, :]
    causal = (jnp.arange(steps)[None, :] <= jnp.arange(steps)[:, None])[:, None, None, None, :]
    s_cache = jnp.where(valid, s_cache, -1e30)
    s_new = jnp.where(causal, s_new, -1e30)
    top = jnp.maximum(jnp.max(s_cache, axis=-1), jnp.max(s_new, axis=-1))[..., None]
    e_cache = jnp.where(valid, jnp.exp(s_cache - top), 0.0)
    e_new = jnp.where(causal, jnp.exp(s_new - top), 0.0)
    total = jnp.sum(e_cache, axis=-1, keepdims=True) + jnp.sum(e_new, axis=-1, keepdims=True)
    p_cache = (e_cache / total).astype(jnp.bfloat16)
    p_new = (e_new / total).astype(jnp.bfloat16)
    out = jnp.einsum("srhgc,rchd->srhgd", p_cache, vc, preferred_element_type=jnp.float32)
    out = out + jnp.einsum("srhgt,trhd->srhgd", p_new, v_new, preferred_element_type=jnp.float32)
    return out.astype(jnp.bfloat16).reshape(steps * rows, kv_local * group * head_size)


def ring_device(place, n):
    place = place % n
    back = place // (n // 2)
    return (1 - back) * (2 * place) + back * (2 * (n - 1 - place) + 1)


def ring_place(device, n):
    odd = device % 2
    return (1 - odd) * (device // 2) + odd * (n - 1 - device // 2)


def remote(src, dst, send, recv, target):
    return pltpu.make_async_remote_copy(
        src_ref=src,
        dst_ref=dst,
        send_sem=send,
        recv_sem=recv,
        device_id=target,
        device_id_type=pl.DeviceIdType.MESH,
    )


class Ring:
    def __init__(self, n, cuts, x_ref, o_ref, sems):
        self.n, self.cuts, self.x_ref, self.o_ref = n, cuts, x_ref, o_ref
        self.local_sem, self.send_sem, self.recv_sem = sems
        self.me = lax.axis_index("fsdp")
        self.place = ring_place(self.me, n)
        self.ways = (
            ring_device(self.place + 1, n),
            ring_device(self.place + n - 1, n),
        )
        self.rows = x_ref.shape[0] // (2 * cuts)

    def own(self):
        return pltpu.make_async_copy(self.x_ref, self.o_ref.at[self.me], self.local_sem)

    def hop(self, step, cut, way):
        origin = ring_device(self.place + self.n + (step if way else -step), self.n)
        span = pl.ds((way * self.cuts + cut) * self.rows, self.rows)
        land = self.o_ref.at[origin, span]
        return remote(
            self.x_ref.at[span] if step == 0 else land,
            land,
            self.send_sem.at[way, step, cut],
            self.recv_sem.at[way, step, cut],
            {"fsdp": self.ways[way]},
        )

    def arrival(self, step, cut, way):
        ahead = step + 1 if way else -step - 1
        origin = ring_device(self.place + self.n + ahead, self.n)
        span = pl.ds((way * self.cuts + cut) * self.rows, self.rows)
        land = self.o_ref.at[origin, span]
        return remote(
            land,
            land,
            self.send_sem.at[way, step, cut],
            self.recv_sem.at[way, step, cut],
            {"fsdp": self.ways[way]},
        )

    def each(self):
        return [(cut, way) for cut in range(self.cuts) for way in range(2)]

    def step(self, step):
        for cut, way in self.each():
            if step > 0:
                self.arrival(step - 1, cut, way).wait_recv()
            if step < self.n - 1:
                self.hop(step, cut, way).start()

    def finish(self):
        self.step(self.n - 1)
        for step in range(self.n - 1):
            for cut, way in self.each():
                self.hop(step, cut, way).wait_send()
        self.own().wait()


def ring_sems(n, cuts):
    return [
        pltpu.SemaphoreType.DMA,
        pltpu.SemaphoreType.DMA((2, n - 1, cuts)),
        pltpu.SemaphoreType.DMA((2, n - 1, cuts)),
    ]


def ring_kernel(n, cuts, x_ref, o_ref, *sems):
    ring = Ring(n, cuts, x_ref, o_ref, sems)
    barrier = pltpu.get_barrier_semaphore()
    for way in ring.ways:
        pl.semaphore_signal(
            barrier, inc=1, device_id={"fsdp": way}, device_id_type=pl.DeviceIdType.MESH
        )
    pl.semaphore_wait(barrier, 2)
    ring.own().start()
    for step in range(n - 1):
        ring.step(step)
    ring.finish()


def ring_gather(shard, n, collective_id, cuts=2):
    return pl.pallas_call(
        functools.partial(ring_kernel, n, cuts),
        out_shape=jax.ShapeDtypeStruct((n,) + shard.shape, shard.dtype),
        in_specs=[pl.BlockSpec(memory_space=pl.ANY)],
        out_specs=pl.BlockSpec(memory_space=pl.ANY),
        scratch_shapes=ring_sems(n, cuts),
        cost_estimate=pl.CostEstimate(
            flops=0, bytes_accessed=shard.size * n * 20, transcendentals=0
        ),
        compiler_params=pltpu.CompilerParams(
            collective_id=collective_id, has_side_effects=True
        ),
    )(shard)


def exchange_kernel(
    n, m, cuts, w_ref, a_ref, w_all, a_row, a_col, ring_local, ring_send, ring_recv,
    local, head_send, head_recv, part_send, part_recv, share_send, share_recv,
):
    f, t = lax.axis_index("fsdp"), lax.axis_index("tp")
    ring = Ring(n, cuts, w_ref, w_all, (ring_local, ring_send, ring_recv))
    barrier = pltpu.get_barrier_semaphore()
    for k in range(1, n):
        pl.semaphore_signal(
            barrier, inc=1, device_id={"fsdp": (f + k) % n},
            device_id_type=pl.DeviceIdType.MESH,
        )
    for k in range(1, m):
        pl.semaphore_signal(
            barrier, inc=1, device_id={"tp": (t + k) % m},
            device_id_type=pl.DeviceIdType.MESH,
        )
    pl.semaphore_wait(barrier, n + m - 2)
    tokens, heads = a_ref.shape
    wide = a_col.shape[2]
    part = tokens // m

    def columns(owner):
        return a_row.at[:, pl.ds(pl.multiple_of(owner * heads, 128), heads)]

    def piece(target):
        return a_row.at[
            pl.ds(pl.multiple_of(t * part, part), part),
            pl.ds(pl.multiple_of(target * wide, 128), wide),
        ]

    def slot(group, quarter):
        return a_col.at[group, pl.ds(pl.multiple_of(quarter * part, part), part)]

    def share(quarter):
        return a_col.at[:, pl.ds(pl.multiple_of(quarter * part, part), part)]

    own_heads = pltpu.make_async_copy(a_ref, columns(t), local.at[0])
    own_heads.start()
    for k in range(1, m):
        remote(
            a_ref, columns(t), head_send.at[k - 1], head_recv.at[k - 1],
            {"tp": (t + k) % m},
        ).start()
    ring.own().start()
    ring.step(0)
    own_heads.wait()
    for k in range(1, m):
        land = columns((t + m - k) % m)
        remote(
            land, land, head_send.at[k - 1], head_recv.at[k - 1], {"tp": (t + k) % m}
        ).wait_recv()
    own_part = pltpu.make_async_copy(piece(f), slot(f, t), local.at[1])
    own_part.start()
    for k in range(1, n):
        remote(
            piece((f + k) % n), slot(f, t), part_send.at[k - 1], part_recv.at[k - 1],
            {"fsdp": (f + k) % n},
        ).start()
    ring.step(1)
    own_part.wait()
    for k in range(1, n):
        land = slot((f + n - k) % n, t)
        remote(
            land, land, part_send.at[k - 1], part_recv.at[k - 1],
            {"fsdp": (f + k) % n},
        ).wait_recv()
    for k in range(1, m):
        remote(
            share(t), share(t), share_send.at[k - 1], share_recv.at[k - 1],
            {"tp": (t + k) % m},
        ).start()
    for step in range(2, n - 1):
        ring.step(step)
    ring.finish()
    for k in range(1, m):
        land = share((t + m - k) % m)
        remote(
            land, land, share_send.at[k - 1], share_recv.at[k - 1],
            {"tp": (t + k) % m},
        ).wait_recv()
    for k in range(1, m):
        remote(
            a_ref, columns(t), head_send.at[k - 1], head_recv.at[k - 1],
            {"tp": (t + k) % m},
        ).wait_send()
        remote(
            share(t), share(t), share_send.at[k - 1], share_recv.at[k - 1],
            {"tp": (t + k) % m},
        ).wait_send()
    for k in range(1, n):
        remote(
            piece((f + k) % n), slot(f, t), part_send.at[k - 1], part_recv.at[k - 1],
            {"fsdp": (f + k) % n},
        ).wait_send()


def exchange(weights, attended, n, m, collective_id, cuts=2):
    tokens, heads = attended.shape
    dma = pltpu.SemaphoreType.DMA
    return pl.pallas_call(
        functools.partial(exchange_kernel, n, m, cuts),
        out_shape=(
            jax.ShapeDtypeStruct((n,) + weights.shape, weights.dtype),
            jax.ShapeDtypeStruct((tokens, heads * m), attended.dtype),
            jax.ShapeDtypeStruct((n, tokens, heads * m // n), attended.dtype),
        ),
        in_specs=[pl.BlockSpec(memory_space=pl.ANY)] * 2,
        out_specs=[pl.BlockSpec(memory_space=pl.ANY)] * 3,
        scratch_shapes=ring_sems(n, cuts)
        + [dma((2,))]
        + [dma((m - 1,))] * 2
        + [dma((n - 1,))] * 2
        + [dma((m - 1,))] * 2,
        cost_estimate=pl.CostEstimate(
            flops=0, bytes_accessed=weights.size * n * 20, transcendentals=0
        ),
        compiler_params=pltpu.CompilerParams(
            collective_id=collective_id, has_side_effects=True
        ),
    )(weights, attended)


def shards(fsdp, tp, step_input, lengths, cache_k, cache_v, w_query, w_key, w_value, w_output, loss_grad):
    steps, rows, width = step_input.shape
    flat = step_input.reshape(steps * rows, width)
    head_size = HD
    kv_local = w_key.shape[1] // head_size
    q_local = w_query.shape[1] // head_size
    group = q_local // kv_local
    upstream = loss_grad.reshape(steps * rows, loss_grad.shape[2])
    fused = jnp.concatenate([w_query, w_key, w_value], axis=1)
    weights, upstream = lax.optimization_barrier((ring_gather(fused, fsdp, 0), upstream))
    weights = weights.reshape(width, fused.shape[1])
    grad_whole = lax.all_gather(upstream, "fsdp", axis=0, tiled=True)
    projection = jnp.dot(flat, weights, preferred_element_type=jnp.float32)
    query, key, value = jnp.split(
        projection, (w_query.shape[1], w_query.shape[1] + w_key.shape[1]), axis=1
    )
    pos = lengths.astype(jnp.float32)[None, :] + jnp.arange(steps).astype(jnp.float32)[:, None]
    q_rot = rotate(query.reshape(steps, rows, q_local, head_size), pos[:, :, None]).astype(
        jnp.bfloat16
    )
    k_new = rotate(key.reshape(steps, rows, kv_local, head_size), pos[:, :, None]).astype(
        jnp.bfloat16
    )
    v_new = value.reshape(steps, rows, kv_local, head_size).astype(jnp.bfloat16)
    local_attended = attend(q_rot, k_new, v_new, cache_k, cache_v, lengths, kv_local, group)
    out_whole, attended, swapped = exchange(w_output, local_attended, fsdp, tp, 1)
    out_whole = out_whole.reshape(attended.shape[1], w_output.shape[1])
    swapped = swapped.reshape(fsdp * steps * rows, swapped.shape[2])
    projected = jnp.dot(attended, out_whole, preferred_element_type=jnp.float32)
    layer_out = projected.astype(jnp.bfloat16).reshape(steps, rows, w_output.shape[1])
    grad_output = lax.dot_general(
        swapped, grad_whole, (((0,), (0,)), ((), ())), preferred_element_type=jnp.float32
    )
    return (layer_out, grad_output)


def solution(mesh):
    in_specs = (
        P(None, "fsdp", None),
        P("fsdp"),
        P("fsdp", None, "tp"),
        P("fsdp", None, "tp"),
        P("fsdp", "tp"),
        P("fsdp", "tp"),
        P("fsdp", "tp"),
        P("fsdp", "tp"),
        P(None, "fsdp", "tp"),
    )
    out_specs = (P(None, "fsdp", "tp"), P("fsdp", "tp"))
    body = functools.partial(shards, mesh.shape["fsdp"], mesh.shape["tp"])
    return jax.shard_map(body, mesh=mesh, in_specs=in_specs, out_specs=out_specs, check_vma=False)
```

```python
import functools

import jax
import jax.numpy as jnp
from jax import lax
from jax.experimental import pallas as pl
from jax.experimental.pallas import tpu as pltpu
from jax.sharding import PartitionSpec as P

HD = 128


rope_base = 1000000.0


def rotate(vec, pos):
    half = vec.shape[-1] // 2
    freq = rope_base ** (-(jnp.arange(half).astype(jnp.float32) * 2.0) / vec.shape[-1])
    angle = pos[..., None] * freq
    cosine = jnp.cos(angle)
    sine = jnp.sin(angle)
    first = vec[..., :half]
    second = vec[..., half:]
    return jnp.concatenate(
        [first * cosine - second * sine, second * cosine + first * sine], axis=-1
    )


def attend(q_rot, k_new, v_new, cache_k, cache_v, lengths, kv_local, group):
    steps, rows = (q_rot.shape[0], q_rot.shape[1])
    head_size = q_rot.shape[-1]
    cache_len = cache_k.shape[1]
    qg = q_rot.reshape(steps, rows, kv_local, group, head_size)
    kc = cache_k.reshape(rows, cache_len, kv_local, head_size)
    vc = cache_v.reshape(rows, cache_len, kv_local, head_size)
    scale = 1.0 / head_size**0.5
    s_cache = jnp.einsum("srhgd,rchd->srhgc", qg, kc, preferred_element_type=jnp.float32) * scale
    s_new = jnp.einsum("srhgd,trhd->srhgt", qg, k_new, preferred_element_type=jnp.float32) * scale
    valid = (jnp.arange(cache_len)[None, :] < lengths[:, None])[None, :, None, None, :]
    causal = (jnp.arange(steps)[None, :] <= jnp.arange(steps)[:, None])[:, None, None, None, :]
    s_cache = jnp.where(valid, s_cache, -1e30)
    s_new = jnp.where(causal, s_new, -1e30)
    top = jnp.maximum(jnp.max(s_cache, axis=-1), jnp.max(s_new, axis=-1))[..., None]
    e_cache = jnp.where(valid, jnp.exp(s_cache - top), 0.0)
    e_new = jnp.where(causal, jnp.exp(s_new - top), 0.0)
    total = jnp.sum(e_cache, axis=-1, keepdims=True) + jnp.sum(e_new, axis=-1, keepdims=True)
    p_cache = (e_cache / total).astype(jnp.bfloat16)
    p_new = (e_new / total).astype(jnp.bfloat16)
    out = jnp.einsum("srhgc,rchd->srhgd", p_cache, vc, preferred_element_type=jnp.float32)
    out = out + jnp.einsum("srhgt,trhd->srhgd", p_new, v_new, preferred_element_type=jnp.float32)
    return out.astype(jnp.bfloat16).reshape(steps * rows, kv_local * group * head_size)


def ring_device(place, n):
    place = place % n
    back = place // (n // 2)
    return (1 - back) * (2 * place) + back * (2 * (n - 1 - place) + 1)


def ring_place(device, n):
    odd = device % 2
    return (1 - odd) * (device // 2) + odd * (n - 1 - device // 2)


def remote(src, dst, send, recv, target):
    return pltpu.make_async_remote_copy(
        src_ref=src,
        dst_ref=dst,
        send_sem=send,
        recv_sem=recv,
        device_id=target,
        device_id_type=pl.DeviceIdType.MESH,
    )


class Ring:
    def __init__(self, n, cuts, x_ref, o_ref, sems, early=()):
        self.early, self.begin = early, len(early)
        self.n, self.cuts, self.x_ref, self.o_ref = n, cuts, x_ref, o_ref
        self.local_sem, self.send_sem, self.recv_sem = sems
        self.me = lax.axis_index("fsdp")
        self.place = ring_place(self.me, n)
        self.ways = (
            ring_device(self.place + 1, n),
            ring_device(self.place + n - 1, n),
        )
        self.rows = x_ref.shape[0] // (2 * cuts)

    def own(self):
        return pltpu.make_async_copy(self.x_ref, self.o_ref.at[self.me], self.local_sem)

    def hop(self, step, cut, way):
        origin = ring_device(self.place + self.n + (step if way else -step), self.n)
        span = pl.ds((way * self.cuts + cut) * self.rows, self.rows)
        land = self.o_ref.at[origin, span]
        source = self.x_ref.at[span] if step == 0 else land
        if step == self.begin and step > 0:
            source = self.early[step - 1][way].at[pl.ds(cut * self.rows, self.rows)]
        return remote(
            source,
            land,
            self.send_sem.at[way, step, cut],
            self.recv_sem.at[way, step, cut],
            {"fsdp": self.ways[way]},
        )

    def arrival(self, step, cut, way):
        ahead = step + 1 if way else -step - 1
        origin = ring_device(self.place + self.n + ahead, self.n)
        span = pl.ds((way * self.cuts + cut) * self.rows, self.rows)
        land = self.o_ref.at[origin, span]
        return remote(
            land,
            land,
            self.send_sem.at[way, step, cut],
            self.recv_sem.at[way, step, cut],
            {"fsdp": self.ways[way]},
        )

    def keep(self, sem):
        copies = [pltpu.make_async_copy(self.x_ref, self.o_ref.at[self.me], sem.at[0, 0])]
        for step, pair in enumerate(self.early):
            for way in range(2):
                ahead = step + 1 if way else -step - 1
                origin = ring_device(self.place + self.n + ahead, self.n)
                span = pl.ds(way * self.cuts * self.rows, self.cuts * self.rows)
                copies.append(
                    pltpu.make_async_copy(
                        pair[way], self.o_ref.at[origin, span], sem.at[step + 1, way]
                    )
                )
        return copies

    def each(self):
        return [(cut, way) for cut in range(self.cuts) for way in range(2)]

    def step(self, step):
        for cut, way in self.each():
            if step > self.begin:
                self.arrival(step - 1, cut, way).wait_recv()
            if step < self.n - 1:
                self.hop(step, cut, way).start()

    def finish(self):
        for step in range(self.begin, self.n - 1):
            for cut, way in self.each():
                self.hop(step, cut, way).wait_send()


def ring_sems(n, cuts):
    return [
        pltpu.SemaphoreType.DMA,
        pltpu.SemaphoreType.DMA((2, n - 1, cuts)),
        pltpu.SemaphoreType.DMA((2, n - 1, cuts)),
    ]


def ring_kernel(n, cuts, x_ref, o_ref, *sems):
    ring = Ring(n, cuts, x_ref, o_ref, sems)
    barrier = pltpu.get_barrier_semaphore()
    for way in ring.ways:
        pl.semaphore_signal(
            barrier, inc=1, device_id={"fsdp": way}, device_id_type=pl.DeviceIdType.MESH
        )
    pl.semaphore_wait(barrier, 2)
    ring.own().start()
    for step in range(n - 1):
        ring.step(step)
    ring.step(n - 1)
    ring.finish()
    ring.own().wait()


def ring_gather(shard, n, collective_id, cuts=2):
    return pl.pallas_call(
        functools.partial(ring_kernel, n, cuts),
        out_shape=jax.ShapeDtypeStruct((n,) + shard.shape, shard.dtype),
        in_specs=[pl.BlockSpec(memory_space=pl.ANY)],
        out_specs=pl.BlockSpec(memory_space=pl.ANY),
        scratch_shapes=ring_sems(n, cuts),
        cost_estimate=pl.CostEstimate(
            flops=0, bytes_accessed=shard.size * n * 20, transcendentals=0
        ),
        compiler_params=pltpu.CompilerParams(
            collective_id=collective_id, has_side_effects=True
        ),
    )(shard)


def exchange_kernel(n, m, cuts, early, w_ref, g_ref, a_ref, *refs):
    w_early = [refs[2 * k : 2 * k + 2] for k in range(early)]
    g_early = [refs[2 * k : 2 * k + 2] for k in range(early, 2 * early)]
    (
        out_ref, w_all, g_all, a_row, a_col,
        ring_local, ring_send, ring_recv, g_local, g_send, g_recv,
        local, head_send, head_recv, part_send, part_recv, share_send, share_recv,
        held, block, total, load, keep_sem,
    ) = refs[4 * early :]
    f, t = lax.axis_index("fsdp"), lax.axis_index("tp")
    ring = Ring(n, cuts, w_ref, w_all, (ring_local, ring_send, ring_recv), w_early)
    ring_g = Ring(n, cuts, g_ref, g_all, (g_local, g_send, g_recv), g_early)
    barrier = pltpu.get_barrier_semaphore()
    for k in range(1, n):
        pl.semaphore_signal(
            barrier, inc=1, device_id={"fsdp": (f + k) % n},
            device_id_type=pl.DeviceIdType.MESH,
        )
    for k in range(1, m):
        pl.semaphore_signal(
            barrier, inc=1, device_id={"tp": (t + k) % m},
            device_id_type=pl.DeviceIdType.MESH,
        )
    pl.semaphore_wait(barrier, n + m - 2)
    tokens, heads = a_ref.shape
    wide = a_col.shape[2]
    part = tokens // m

    def columns(owner):
        return a_row.at[:, pl.ds(pl.multiple_of(owner * heads, 128), heads)]

    def piece(target):
        return a_row.at[
            pl.ds(pl.multiple_of(t * part, part), part),
            pl.ds(pl.multiple_of(target * wide, 128), wide),
        ]

    def slot(group, quarter):
        return a_col.at[group, pl.ds(pl.multiple_of(quarter * part, part), part)]

    def share(quarter):
        return a_col.at[:, pl.ds(pl.multiple_of(quarter * part, part), part)]

    half = w_ref.shape[0] // 2
    tile = min(512, total.shape[1])

    def multiply(origin, sources):
        copies = [
            pltpu.make_async_copy(source, block.at[way], load.at[way])
            for way, source in enumerate(sources)
        ]
        for copy in copies:
            copy.start()
        for way, copy in enumerate(copies):
            copy.wait()
            depth = pl.ds(
                pl.multiple_of(origin[way] * 2 * half + way * half, 128), half
            )

            @pl.loop(0, total.shape[1] // tile)
            def _(j):
                span = pl.ds(pl.multiple_of(j * tile, 128), tile)
                total[:, span] += jnp.dot(
                    held[:, depth], block[way, :, span],
                    preferred_element_type=jnp.float32,
                )

    def arrived(step):
        ends = [
            ring_device(ring.place + n + (step + 1 if way else -step - 1), n)
            for way in range(2)
        ]
        if step < early:
            return ends, w_early[step]
        return ends, [
            w_all.at[end, pl.ds(way * half, half)] for way, end in enumerate(ends)
        ]

    own_heads = pltpu.make_async_copy(a_ref, columns(t), local.at[0])
    own_heads.start()
    for k in range(1, m):
        remote(
            a_ref, columns(t), head_send.at[k - 1], head_recv.at[k - 1],
            {"tp": (t + k) % m},
        ).start()
    ring.step(early)
    ring_g.step(early)
    kept = ring_g.keep(keep_sem)
    for copy in kept:
        copy.start()
    own_heads.wait()
    for k in range(1, m):
        land = columns((t + m - k) % m)
        remote(
            land, land, head_send.at[k - 1], head_recv.at[k - 1], {"tp": (t + k) % m}
        ).wait_recv()
    own_part = pltpu.make_async_copy(piece(f), slot(f, t), local.at[1])
    own_part.start()
    for k in range(1, n):
        remote(
            piece((f + k) % n), slot(f, t), part_send.at[k - 1], part_recv.at[k - 1],
            {"fsdp": (f + k) % n},
        ).start()
    rows_in = pltpu.make_async_copy(a_row, held, local.at[2])
    rows_in.start()
    total[...] = jnp.zeros_like(total)
    rows_in.wait()
    multiply([f, f], [w_ref.at[pl.ds(way * half, half)] for way in range(2)])
    for step in range(early):
        multiply(*arrived(step))
    own_part.wait()
    for k in range(1, n):
        land = slot((f + n - k) % n, t)
        remote(
            land, land, part_send.at[k - 1], part_recv.at[k - 1],
            {"fsdp": (f + k) % n},
        ).wait_recv()
    for k in range(1, m):
        remote(
            share(t), share(t), share_send.at[k - 1], share_recv.at[k - 1],
            {"tp": (t + k) % m},
        ).start()
    for step in range(early + 1, n):
        ring.step(step)
        ring_g.step(step)
        multiply(*arrived(step - 1))
    out_ref[...] = total[...].astype(out_ref.dtype)
    ring.finish()
    ring_g.finish()
    for copy in kept:
        copy.wait()
    for k in range(1, m):
        land = share((t + m - k) % m)
        remote(
            land, land, share_send.at[k - 1], share_recv.at[k - 1],
            {"tp": (t + k) % m},
        ).wait_recv()
    for k in range(1, m):
        remote(
            a_ref, columns(t), head_send.at[k - 1], head_recv.at[k - 1],
            {"tp": (t + k) % m},
        ).wait_send()
        remote(
            share(t), share(t), share_send.at[k - 1], share_recv.at[k - 1],
            {"tp": (t + k) % m},
        ).wait_send()
    for k in range(1, n):
        remote(
            piece((f + k) % n), slot(f, t), part_send.at[k - 1], part_recv.at[k - 1],
            {"fsdp": (f + k) % n},
        ).wait_send()


def exchange(weights, upstream, attended, w_early, g_early, n, m, collective_id, cuts=2):
    tokens, heads = attended.shape
    half, wide = weights.shape[0] // 2, weights.shape[1]
    early = len(w_early)
    dma = pltpu.SemaphoreType.DMA
    anywhere = pl.BlockSpec(memory_space=pl.ANY)
    out, _, grad_whole, _, swapped = pl.pallas_call(
        functools.partial(exchange_kernel, n, m, cuts, early),
        out_shape=(
            jax.ShapeDtypeStruct((tokens, wide), attended.dtype),
            jax.ShapeDtypeStruct((n,) + weights.shape, weights.dtype),
            jax.ShapeDtypeStruct((n,) + upstream.shape, upstream.dtype),
            jax.ShapeDtypeStruct((tokens, heads * m), attended.dtype),
            jax.ShapeDtypeStruct((n, tokens, heads * m // n), attended.dtype),
        ),
        in_specs=[anywhere] * (3 + 4 * early),
        out_specs=[pl.BlockSpec(memory_space=pltpu.VMEM)] + [anywhere] * 4,
        scratch_shapes=ring_sems(n, cuts) * 2
        + [dma((3,))]
        + [dma((m - 1,))] * 2
        + [dma((n - 1,))] * 2
        + [dma((m - 1,))] * 2
        + [
            pltpu.VMEM((tokens, heads * m), attended.dtype),
            pltpu.VMEM((2, half, wide), weights.dtype),
            pltpu.VMEM((tokens, wide), jnp.float32),
            dma((2,)),
            dma((early + 1, 2)),
        ],
        cost_estimate=pl.CostEstimate(
            flops=0, bytes_accessed=weights.size * n * 20, transcendentals=0
        ),
        compiler_params=pltpu.CompilerParams(
            collective_id=collective_id,
            has_side_effects=True,
            vmem_limit_bytes=32 * 1024 * 1024,
        ),
    )(weights, upstream, attended, *sum(w_early, ()), *sum(g_early, ()))
    return out, grad_whole, swapped


def shards(fsdp, tp, step_input, lengths, cache_k, cache_v, w_query, w_key, w_value, w_output, loss_grad):
    steps, rows, width = step_input.shape
    flat = step_input.reshape(steps * rows, width)
    head_size = HD
    kv_local = w_key.shape[1] // head_size
    q_local = w_query.shape[1] // head_size
    group = q_local // kv_local
    upstream = loss_grad.reshape(steps * rows, loss_grad.shape[2])
    fused = jnp.concatenate([w_query, w_key, w_value], axis=1)
    w_halves, g_halves = tuple(jnp.split(w_output, 2)), tuple(jnp.split(upstream, 2))
    weights, w_halves, g_halves = lax.optimization_barrier(
        (ring_gather(fused, fsdp, 0), w_halves, g_halves)
    )
    order = [ring_device(place, fsdp) for place in range(fsdp)]
    after = order[1:] + order[:1]
    pairs = (list(zip(order, after)), list(zip(after, order)))
    w_early, g_early = [], []
    for _ in range(2):
        w_halves = tuple(lax.ppermute(h, "fsdp", p) for h, p in zip(w_halves, pairs))
        g_halves = tuple(lax.ppermute(h, "fsdp", p) for h, p in zip(g_halves, pairs))
        w_early.append(w_halves)
        g_early.append(g_halves)
    weights = weights.reshape(width, fused.shape[1])
    projection = jnp.dot(flat, weights, preferred_element_type=jnp.float32)
    query, key, value = jnp.split(
        projection, (w_query.shape[1], w_query.shape[1] + w_key.shape[1]), axis=1
    )
    pos = lengths.astype(jnp.float32)[None, :] + jnp.arange(steps).astype(jnp.float32)[:, None]
    q_rot = rotate(query.reshape(steps, rows, q_local, head_size), pos[:, :, None]).astype(
        jnp.bfloat16
    )
    k_new = rotate(key.reshape(steps, rows, kv_local, head_size), pos[:, :, None]).astype(
        jnp.bfloat16
    )
    v_new = value.reshape(steps, rows, kv_local, head_size).astype(jnp.bfloat16)
    local_attended = attend(q_rot, k_new, v_new, cache_k, cache_v, lengths, kv_local, group)
    layer_out, grad_whole, swapped = exchange(
        w_output, upstream, local_attended, w_early, g_early, fsdp, tp, 1
    )
    grad_whole = grad_whole.reshape(fsdp * steps * rows, upstream.shape[1])
    layer_out = layer_out.reshape(steps, rows, w_output.shape[1])
    swapped = swapped.reshape(fsdp * steps * rows, swapped.shape[2])
    grad_output = lax.dot_general(
        swapped, grad_whole, (((0,), (0,)), ((), ())), preferred_element_type=jnp.float32
    )
    return (layer_out, grad_output)


def solution(mesh):
    in_specs = (
        P(None, "fsdp", None),
        P("fsdp"),
        P("fsdp", None, "tp"),
        P("fsdp", None, "tp"),
        P("fsdp", "tp"),
        P("fsdp", "tp"),
        P("fsdp", "tp"),
        P("fsdp", "tp"),
        P(None, "fsdp", "tp"),
    )
    out_specs = (P(None, "fsdp", "tp"), P("fsdp", "tp"))
    body = functools.partial(shards, mesh.shape["fsdp"], mesh.shape["tp"])
    return jax.shard_map(body, mesh=mesh, in_specs=in_specs, out_specs=out_specs, check_vma=False)
```
